512 devices in a mesh: lon: 64 (over z_hi, y, core), lat: 8 (over x, z_lo).
Axes of the slice: x: 4, y: 8, z: 8 (z_hi: 4, z_lo: 2; z = z_hi * 2 + z_lo), core: 2. Of those that a mesh axis runs over, the one named last changes fastest.
Arguments:
- zonal: float32 [512, 128], P('lon', 'lat'), may hold values from -0.9 to 0.9
- merid: float32 [512, 128], P('lon', 'lat'), may hold values from -0.9 to 0.9
- diffuse: float32 [512, 128], P('lon', 'lat'), may hold values from 0.02 to 0.2
- coupling: float32 [360, 360], replicated, may hold values from -0.25 to 0.25
- table: float32 [128, 360], replicated, may hold values from -6 to 6
- obs_dep: float32 [2, 131072], P(None, ('lon', 'lat')), may hold values from -6 to 6
- obs_frac: float32 [2, 131072, 2], P(None, ('lon', 'lat')), may hold values from 0 to 1
- obs_owner: int32 [2, 131072, 1], P(None, ('lon', 'lat')), may hold values from 0 to 63; in each aligned block of 256 rows (0 to 255, 256 to 511, ..., all dimensions but the last counted through in order) at most 8 rows name the same one
- obs_lon: int32 [2, 131072], P(None, ('lon', 'lat')), may hold values from 0 to 7
- obs_lat: int32 [2, 131072], P(None, ('lon', 'lat')), may hold values from 0 to 14
- obs_chan: int32 [2, 131072], P(None, ('lon', 'lat')), may hold values from 0 to 127
Outputs:
- adjoint_field: float32 [512, 46080], P('lon', 'lat')
The draws below stay inside these ranges and needn't reach their ends.
Inputs may be any that keep to these rules, and one draw needn't show every extreme that they name: `obs_owner`: in each step, the rows of one device (aligned blocks of 256 rows) name any longitude block at most 8 times, and some block exactly 8 times. `obs_lat`: A base cell is never the last row of its band.
All inputs are finite; a program needn't handle non-finite values.
Results may differ from the reference program's by a relative error of at most 0.00011.
Values sent between devices are 32-bit elements; how exact they have to be, the bound alone decides.
A program may use at most 64 MiB of HBM per device.

```python
import math
import jax
import jax.numpy as jnp
import numpy as np
from jax import lax

FIELDS = 5
LEV = 72
NCHAN = 128
STEPS = 2
LON_DEV = 8
LAT_DEV = 16
CAP = 8
FL = 360
NLON = 512
NLAT = 128
OBS_DEV = 256
NOBS = 131072
N_LON = 64
N_LAT = 8


def with_ends(array, key, smallest, high):
    longest = array.shape.index(max(array.shape))
    spots = []
    for shift in (0, 1):
        where = [jax.random.randint(jax.random.fold_in(key, axis), (), 0, length) for axis, length in enumerate(array.shape)]
        where[longest] = (where[longest] + shift) % array.shape[longest]
        spots.append(tuple(where))
    return array.at[spots[0]].set(smallest).at[spots[1]].set(high)


def steps_of(stream_key, extent, shards, low, top_value):
    loudness = 1.0
    for dim, blocks in shards:
        steps = jax.random.uniform(jax.random.fold_in(jax.random.fold_in(stream_key, 6), dim), (blocks,), jnp.float32, low / len(shards), top_value / len(shards))
        loudness = loudness * jnp.repeat(jnp.exp(steps), extent[dim] // blocks).reshape((-1,) + (1,) * (len(extent) - 1 - dim))
    return loudness


def shared_out(stream_key, own, number, rows, number_of, top, reach, slope):
    ranking = jax.random.permutation(stream_key, number_of)
    crowded, ordinary = shares(number_of, rows * top, reach, slope, True), shares(number_of, rows * top, reach, slope, False)
    places = jnp.arange(number_of)

    def named(sizes, rotation):
        used = int((sizes > 0).sum())
        fixed = max(1, used // 4)
        moved = fixed + (places - fixed + rotation * (used - fixed)) % max(1, number_of - fixed)
        return jnp.zeros((number_of,), jnp.int32).at[ranking[jnp.where(places < fixed, places, moved)]].set(jnp.asarray(sizes, jnp.int32))

    sizes = jnp.where(number % 4 == 0, named(crowded, number // 4), named(ordinary, number - number // 4 - 1))
    mixed = jax.random.permutation(jax.random.fold_in(own, 3), number_of)
    source_of, sink = mixed[0:number_of // 2 * 2:2], mixed[1:number_of // 2 * 2:2]
    margin = jnp.minimum(sizes[source_of] - 1, reach - sizes[sink]) // 2
    margin = jnp.where((source_of == ranking[0]) | (sink == ranking[0]) | (sizes[sink] == 0), 0, jnp.maximum(margin, 0))
    moved = jax.random.randint(jax.random.fold_in(own, 4), (number_of // 2,), 0, 1 << 20) % (margin + 1)
    sizes = sizes.at[source_of].add(-moved).at[sink].add(moved)
    members = jnp.searchsorted(jnp.cumsum(sizes), jnp.arange(rows * top), side="right").astype(jnp.int32)
    table = members.reshape(top, rows).T
    table = table[jax.random.permutation(jax.random.fold_in(own, 1), rows)]
    rotation = jax.random.randint(jax.random.fold_in(own, 2), (rows, 1), 0, top)
    return jnp.take_along_axis(table, (jnp.arange(top)[None, :] + rotation) % top, axis=1)


def shares(count, total, limit, slope, full):
    portions = [(1 << 20) // math.isqrt(grade ** slope) + 1 for grade in range(1, count + 1)]
    largest = limit if full else min(limit, max(-(-total // count), total * portions[0] // sum(portions)))
    least = 1 if total - largest >= count - 1 else 0
    given, surplus = [largest] + [least] * (count - 1), total - largest - least * (count - 1)
    while surplus > 0:
        free = [i for i in range(1, count) if given[i] < largest] or [i for i in range(1, count) if given[i] < limit]
        mass, remaining = sum([portions[i] for i in free]), surplus
        for i in free:
            more = min(limit - given[i], max(1, remaining * portions[i] // mass), surplus)
            given[i] = given[i] + more
            surplus = surplus - more
    return np.array(given)


def gaussian(stream_key, extent, deviation, most, cuts=(), kind=jnp.bfloat16):
    array = deviation * jax.random.normal(stream_key, extent, jnp.float32)
    if cuts:
        array = array * steps_of(stream_key, extent, cuts, -0.22, 0.18)
    return jnp.clip(array, -most, most).astype(kind)


def setup_inputs(seed: int = 0) -> dict:
    seeds = jax.random.split(jax.random.key(seed), 12)
    zonal = jnp.clip(jax.random.uniform(seeds[0], (NLON, NLAT), jnp.float32, -0.9, 0.9) * steps_of(seeds[0], (NLON, NLAT), ((0, 64), (1, 8)), -0.4, 0.0), -0.9, 0.9)
    merid = jnp.clip(jax.random.uniform(seeds[1], (NLON, NLAT), jnp.float32, -0.9, 0.9) * steps_of(seeds[1], (NLON, NLAT), ((0, 64), (1, 8)), -0.4, 0.0), -0.9, 0.9)
    diffuse = jnp.clip(jnp.exp(math.log(0.2) - 2.3025851 * jax.random.uniform(seeds[2], (NLON, NLAT), jnp.float32) ** steps_of(seeds[2], (NLON, NLAT), ((0, 64), (1, 8)), -0.2, 0.2)), 0.02, 0.2)
    coupling = gaussian(seeds[3], (FL, FL), 0.04, 0.25, (), jnp.float32)
    table = gaussian(seeds[4], (NCHAN, FL), 1.0, 6.0, (), jnp.float32)
    obs_dep = gaussian(seeds[5], (STEPS, NOBS), 1.0, 6.0, ((1, 512),), jnp.float32)
    obs_frac = jnp.clip(1.0 * jax.random.uniform(seeds[6], (STEPS, NOBS, 2), jnp.float32) ** steps_of(seeds[6], (STEPS, NOBS, 2), ((1, 512),), -0.2, 0.2), 0.0, 1.0)
    obs_owner_keys = jax.random.split(jax.random.fold_in(seeds[7], 1), STEPS * NOBS // OBS_DEV)
    obs_owner_turns = jax.random.permutation(jax.random.fold_in(seeds[7], 3), STEPS * NOBS // OBS_DEV)
    obs_owner = jax.vmap(lambda own, number: shared_out(jax.random.fold_in(seeds[7], 2), own, number, OBS_DEV, N_LON, 1, CAP, 2))(obs_owner_keys, obs_owner_turns).reshape((STEPS, NOBS, 1))
    obs_lon = with_ends(jax.random.randint(seeds[8], (STEPS, NOBS), 0, LON_DEV), jax.random.fold_in(seeds[8], 1), 0, LON_DEV - 1).astype(jnp.int32)
    obs_lat = with_ends(jax.random.randint(seeds[9], (STEPS, NOBS), 0, LAT_DEV - 1), jax.random.fold_in(seeds[9], 1), 0, (LAT_DEV - 1) - 1).astype(jnp.int32)
    obs_chan = with_ends(jax.random.randint(seeds[10], (STEPS, NOBS), 0, NCHAN), jax.random.fold_in(seeds[10], 1), 0, NCHAN - 1).astype(jnp.int32)
    return dict(zonal=zonal, merid=merid, diffuse=diffuse, coupling=coupling, table=table, obs_dep=obs_dep, obs_frac=obs_frac, obs_owner=obs_owner, obs_lon=obs_lon, obs_lat=obs_lat, obs_chan=obs_chan)


HALF_ROOT = 0.7071067811865476


def latitude_response(circle_len, lat_rows):
    row_ids = jnp.arange(lat_rows, dtype=jnp.float32)
    coslat = jnp.cos((row_ids + 0.5) * (math.pi / lat_rows) - 0.5 * math.pi)
    wavenum = jnp.arange(circle_len // 2 + 1, dtype=jnp.float32)
    sines = jnp.sin(wavenum * (math.pi / circle_len))
    return coslat[None, :] / jnp.maximum(HALF_ROOT * sines[:, None], coslat[None, :])


def obs_forcing(step_id, table, obs_dep, obs_frac, obs_owner, obs_lon, obs_lat, obs_chan):
    row_ids = jnp.arange(obs_dep.shape[1], dtype=jnp.int32)
    bands = (row_ids // OBS_DEV) % N_LAT
    west_lon = obs_owner[step_id, :, 0] * LON_DEV + obs_lon[step_id]
    east_lon = (west_lon + 1) % NLON
    south_lat = bands * LAT_DEV + obs_lat[step_id]
    north_lat = south_lat + 1
    column_vals = obs_dep[step_id][:, None] * table[obs_chan[step_id]]
    along = obs_frac[step_id, :, 0][:, None]
    across = obs_frac[step_id, :, 1][:, None]
    grid = jnp.zeros((NLON, NLAT, FIELDS * LEV), jnp.float32)
    grid = grid.at[west_lon, south_lat].add(((1.0 - along) * (1.0 - across)) * column_vals)
    grid = grid.at[east_lon, south_lat].add((along * (1.0 - across)) * column_vals)
    grid = grid.at[west_lon, north_lat].add(((1.0 - along) * across) * column_vals)
    grid = grid.at[east_lon, north_lat].add((along * across) * column_vals)
    return grid


def adjoint_stencil(state, zonal, merid, diffuse):
    west_vals = jnp.roll(state, 1, axis=0)
    east_vals = jnp.roll(state, -1, axis=0)
    zero_row = jnp.zeros_like(state[:, :1])
    south_vals = jnp.concatenate([zero_row, state[:, :-1]], axis=1)
    north_vals = jnp.concatenate([state[:, 1:], zero_row], axis=1)
    diffusion = diffuse[:, :, None]
    eastward = 0.5 * zonal[:, :, None]
    northward = 0.5 * merid[:, :, None]
    result = (1.0 - 4.0 * diffusion) * state + (diffusion - eastward) * west_vals
    result = result + (diffusion + eastward) * east_vals
    result = result + (diffusion - northward) * south_vals
    result = result + (diffusion + northward) * north_vals
    return result


def reference(zonal, merid, diffuse, coupling, table, obs_dep, obs_frac, obs_owner, obs_lon, obs_lat, obs_chan):
    response = latitude_response(NLON, NLAT)[:, :, None]
    state = jnp.zeros((NLON, NLAT, FIELDS * LEV), jnp.float32)
    for step_id in reversed(range(STEPS)):
        state = state + obs_forcing(step_id, table, obs_dep, obs_frac, obs_owner, obs_lon, obs_lat, obs_chan)
        spectrum = jnp.fft.rfft(state, axis=0)
        state = jnp.fft.irfft(spectrum * response, n=NLON, axis=0)
        state = state + jnp.einsum("xyf,gf->xyg", state, coupling, precision=lax.Precision.HIGHEST)
        state = adjoint_stencil(state, zonal, merid, diffuse)
    return state.reshape(NLON, NLAT * FIELDS * LEV)
```

```python
import math

import jax
import jax.numpy as jnp
from jax import lax
from jax.sharding import PartitionSpec as P

FIELDS = 5
LEV = 72
NCHAN = 128
LON_DEV = 8
LAT_DEV = 16
CAP = 8
PARTS = 4
SHARE = NCHAN // PARTS
ITEMS = 2 * SHARE


HALF_ROOT = 0.7071067811865476
HIGHEST = lax.Precision.HIGHEST
HIGH = lax.Precision.HIGH


def contract_first(left, right, precision):
    return lax.dot_general(left, right, (((0,), (0,)), ((), ())), precision=precision)


def exchange(value):
    return lax.all_to_all(value, "lon", split_axis=0, concat_axis=0, tiled=True)


def filter_matrix(row, circle, lat_rows):
    nwaves = circle // 2 + 1
    wave_ids = jnp.arange(nwaves, dtype=jnp.int32)[:, None]
    cell_ids = jnp.arange(circle, dtype=jnp.int32)[None, :]
    phase = (wave_ids * cell_ids % circle).astype(jnp.float32) * (2.0 * math.pi / circle)
    basis = jnp.concatenate([jnp.cos(phase), jnp.sin(phase)], axis=0)
    coslat = jnp.cos((row.astype(jnp.float32) + 0.5) * (math.pi / lat_rows) - 0.5 * math.pi)
    sines = jnp.sin(jnp.arange(nwaves, dtype=jnp.float32) * (math.pi / circle))
    response = coslat / jnp.maximum(HALF_ROOT * sines[:, None], coslat)
    edge_wave = (wave_ids == 0) | (wave_ids == circle // 2)
    weight = response * jnp.where(edge_wave, 1.0, 2.0) / circle
    scaled = basis * jnp.concatenate([weight, weight], axis=0)
    return contract_first(basis, scaled, HIGH)


def row_neighbours(value, lon_groups, lat_groups):
    def device(row, part):
        return (row % LAT_DEV * PARTS + part) * lat_groups + row // LAT_DEV

    rows = LAT_DEV * lat_groups
    up = [(device(i, p), device(i + 1, p)) for i in range(rows - 1) for p in range(PARTS)]
    south = lax.ppermute(value, ("lon", "lat"), up)
    north = lax.ppermute(value, ("lon", "lat"), [(b, a) for a, b in up])
    return south, north


def per_device(
    zonal, merid, diffuse, coupling, table, obs_dep, obs_frac, obs_owner, obs_lon, obs_lat, obs_chan
):
    lon_groups = lax.axis_size("lon")
    lat_groups = lax.axis_size("lat")
    columns = FIELDS * LEV
    circle = LON_DEV * lon_groups
    lat_rows = LAT_DEV * lat_groups
    lat_index = lax.axis_index("lat")
    own_row = lat_index * LAT_DEV + lax.axis_index("lon") // PARTS
    matrix = filter_matrix(own_row, circle, lat_rows)

    steps, rows = obs_dep.shape
    dest_ids = jnp.arange(lon_groups, dtype=jnp.int32)
    chosen = (obs_owner == dest_ids).astype(jnp.float32)
    earlier = jnp.arange(rows)[:, None] > jnp.arange(rows)[None, :]
    before = lax.dot_general(
        jnp.broadcast_to(earlier.astype(jnp.float32), (steps, rows, rows)),
        chosen,
        (((2,), (1,)), ((0,), (0,))),
    )
    rank = jnp.sum(before * chosen, axis=2)[:, :, None]
    in_slot = rank == jnp.arange(CAP, dtype=jnp.float32)
    details = [
        obs_dep,
        obs_frac[:, :, 0],
        obs_frac[:, :, 1],
        obs_lon.astype(jnp.float32),
        obs_lat.astype(jnp.float32),
        obs_chan.astype(jnp.float32),
    ]
    slotted = jnp.concatenate([jnp.where(in_slot, d[:, :, None], 0.0) for d in details], axis=2)
    sent = lax.dot_general(chosen, slotted, (((1,), (1,)), ((0,), (0,))), precision=HIGHEST)
    by_row = [jnp.repeat(c.T, PARTS, axis=0) for c in (zonal, merid, diffuse)]
    spare = jnp.zeros((lon_groups, 8), jnp.float32)
    got = exchange(jnp.concatenate([sent[0], sent[1]] + by_row + [spare], axis=1))

    cells = jnp.arange(LAT_DEV * (LON_DEV + 1), dtype=jnp.int32)
    cell_lat = (cells // (LON_DEV + 1)).astype(jnp.float32)
    cell_lon = (cells % (LON_DEV + 1)).astype(jnp.float32)
    items = jnp.arange(PARTS * ITEMS, dtype=jnp.int32)
    item_step = items % ITEMS // SHARE
    item_chan = (items // ITEMS * SHARE + items % SHARE).astype(jnp.float32)
    weights, picks = [], []
    for step_id in range(steps):
        start = step_id * 6 * CAP
        dep, along, across, lon, lat, chan = (
            got[:, start + f * CAP : start + (f + 1) * CAP][:, :, None] for f in range(6)
        )
        lon_part = jnp.where(cell_lon == lon, 1.0 - along, 0.0)
        lon_part = lon_part + jnp.where(cell_lon == lon + 1.0, along, 0.0)
        lat_part = jnp.where(cell_lat == lat, 1.0 - across, 0.0)
        lat_part = lat_part + jnp.where(cell_lat == lat + 1.0, across, 0.0)
        weights.append((lon_part * lat_part).reshape(lon_groups * CAP, -1))
        hit = (item_chan == chan) & (item_step == step_id)
        picks.append(jnp.where(hit, dep, 0.0).reshape(lon_groups * CAP, -1))
    forcing = contract_first(jnp.concatenate(weights), jnp.concatenate(picks), HIGH)

    pieces = forcing.reshape(LAT_DEV, LON_DEV + 1, PARTS, ITEMS).transpose(0, 2, 1, 3)
    pieces = exchange(pieces.reshape(lon_groups, (LON_DEV + 1) * ITEMS))
    edge = jnp.roll(pieces[:, LON_DEV * ITEMS :], 1, axis=0)
    first = pieces[:, :ITEMS] + edge
    circles = jnp.concatenate([first, pieces[:, ITEMS : LON_DEV * ITEMS]], axis=1)
    circles = circles.reshape(circle, ITEMS)
    filtered = jnp.dot(matrix, circles, precision=HIGH)
    early, late = filtered[:, :SHARE], filtered[:, SHARE:]
    south, north = row_neighbours(late, lon_groups, lat_groups)
    first_coef = 12 * CAP
    own_zonal, own_merid, own_diffuse = (
        got[:, first_coef + n * LON_DEV : first_coef + (n + 1) * LON_DEV].reshape(circle, 1)
        for n in range(3)
    )
    moved = (1.0 - 4.0 * own_diffuse) * late
    moved = moved + (own_diffuse - 0.5 * own_zonal) * jnp.roll(late, 1, axis=0)
    moved = moved + (own_diffuse + 0.5 * own_zonal) * jnp.roll(late, -1, axis=0)
    moved = moved + (own_diffuse - 0.5 * own_merid) * south
    moved = moved + (own_diffuse + 0.5 * own_merid) * north
    again = jnp.dot(matrix, moved, precision=HIGH)

    both = jnp.concatenate([early, again], axis=1).reshape(lon_groups, LON_DEV * ITEMS)
    west = jnp.roll(both[:, (LON_DEV - 1) * ITEMS :], 1, axis=0)
    east = jnp.roll(both[:, :ITEMS], -1, axis=0)
    back = exchange(jnp.concatenate([west, both, east], axis=1))
    back = back.reshape(LAT_DEV, PARTS, LON_DEV + 2, ITEMS).transpose(2, 0, 1, 3)
    once = table + lax.dot_general(table, coupling, (((1,), (1,)), ((), ())), precision=HIGHEST)
    twice = once + lax.dot_general(once, coupling, (((1,), (1,)), ((), ())), precision=HIGHEST)
    parts = (once.reshape(PARTS, SHARE, columns), twice.reshape(PARTS, SHARE, columns))
    columns_of = jnp.concatenate(parts, axis=1).reshape(PARTS * ITEMS, columns)
    cube = jnp.dot(
        back.reshape((LON_DEV + 2) * LAT_DEV, PARTS * ITEMS), columns_of, precision=HIGH
    ).reshape(LON_DEV + 2, LAT_DEV, columns)
    inner = cube[1:-1]
    up = [(i, i + 1) for i in range(lat_groups - 1)]
    south = lax.ppermute(inner[:, -1], "lat", up)
    north = lax.ppermute(inner[:, 0], "lat", [(b, a) for a, b in up])
    south = jnp.concatenate([south[:, None], inner[:, :-1]], axis=1)
    north = jnp.concatenate([inner[:, 1:], north[:, None]], axis=1)
    diffusion = diffuse[:, :, None]
    eastward = 0.5 * zonal[:, :, None]
    northward = 0.5 * merid[:, :, None]
    result = (1.0 - 4.0 * diffusion) * inner + (diffusion - eastward) * cube[:-2]
    result = result + (diffusion + eastward) * cube[2:]
    result = result + (diffusion - northward) * south
    result = result + (diffusion + northward) * north
    return result.reshape(LON_DEV, LAT_DEV * columns)


def solution(mesh):
    return jax.shard_map(
        per_device,
        mesh=mesh,
        in_specs=(
            P("lon", "lat"),
            P("lon", "lat"),
            P("lon", "lat"),
            P(),
            P(),
            P(None, ("lon", "lat")),
            P(None, ("lon", "lat"), None),
            P(None, ("lon", "lat"), None),
            P(None, ("lon", "lat")),
            P(None, ("lon", "lat")),
            P(None, ("lon", "lat")),
        ),
        out_specs=P("lon", "lat"),
        check_vma=False,
    )
```

```python
import functools
import math

import jax
import jax.numpy as jnp
from jax import lax
from jax.experimental import pallas as pl
from jax.experimental.pallas import tpu as pltpu
from jax.sharding import PartitionSpec as P

FIELDS = 5
LEV = 72
NCHAN = 128
LON_DEV = 8
LAT_DEV = 16
CAP = 8
PARTS = 4
SHARE = NCHAN // PARTS
ITEMS = 2 * SHARE


HALF_ROOT = 0.7071067811865476
HIGHEST = lax.Precision.HIGHEST


def contract_first(left, right, precision):
    return lax.dot_general(left, right, (((0,), (0,)), ((), ())), precision=precision)


def exchange_kernel(compute, reads, count, *refs):
    sent, extra, got = refs[0], refs[1 : 1 + reads], refs[1 + reads]
    made, (send_sem, recv_sem, own_sem) = refs[2 + reads : -3], refs[-3:]
    me = lax.axis_index("lon")

    def other(shift):
        return lax.rem(me + shift, count)

    barrier = pltpu.get_barrier_semaphore()

    @pl.loop(1, count)
    def _(shift):
        pl.semaphore_signal(
            barrier,
            inc=1,
            device_id={"lon": other(shift)},
            device_id_type=pl.DeviceIdType.MESH,
        )

    own = pltpu.make_async_copy(sent.at[me], got.at[me], own_sem)
    own.start()
    pl.semaphore_wait(barrier, count - 1)

    @pl.loop(1, count)
    def _(shift):
        pltpu.make_async_remote_copy(
            src_ref=sent.at[other(shift)],
            dst_ref=got.at[me],
            send_sem=send_sem,
            recv_sem=recv_sem,
            device_id={"lon": other(shift)},
            device_id_type=pl.DeviceIdType.MESH,
        ).start()

    if compute is not None:
        compute(*extra, *made)
    own.wait()
    everything = pltpu.make_async_remote_copy(
        src_ref=sent.at[pl.ds(0, count - 1)],
        dst_ref=got.at[pl.ds(0, count - 1)],
        send_sem=send_sem,
        recv_sem=recv_sem,
        device_id={"lon": other(1)},
        device_id_type=pl.DeviceIdType.MESH,
    )
    everything.wait()


def exchange(value, number, compute=None, extra=(), made=()):
    count, width = value.shape
    shape = jax.ShapeDtypeStruct((count, 1, width), value.dtype)
    in_vmem = pl.BlockSpec(memory_space=pltpu.VMEM)
    outs = pl.pallas_call(
        functools.partial(exchange_kernel, compute, len(extra), count),
        out_shape=(shape,) + tuple(jax.ShapeDtypeStruct(m, jnp.float32) for m in made),
        in_specs=[in_vmem] * (1 + len(extra)),
        out_specs=(in_vmem,) * (1 + len(made)),
        scratch_shapes=[pltpu.SemaphoreType.DMA] * 3,
        compiler_params=pltpu.CompilerParams(collective_id=number, has_side_effects=True),
    )(value.reshape(count, 1, width), *extra)
    return (outs[0].reshape(count, width),) + tuple(outs[1:])


def filter_factors(row, circle, lat_rows):
    half = circle // 2
    wave_ids = jnp.concatenate([jnp.arange(half + 1), jnp.arange(1, half)])
    cell_ids = jnp.arange(circle, dtype=jnp.int32)
    phase = (wave_ids[:, None] * cell_ids[None, :] % circle).astype(jnp.float32)
    phase = phase * (2.0 * math.pi / circle)
    basis = jnp.where(jnp.arange(circle)[:, None] <= half, jnp.cos(phase), jnp.sin(phase))
    coslat = jnp.cos((row.astype(jnp.float32) + 0.5) * (math.pi / lat_rows) - 0.5 * math.pi)
    sines = jnp.sin(wave_ids.astype(jnp.float32) * (math.pi / circle))
    response = coslat / jnp.maximum(HALF_ROOT * sines, coslat)
    edge_wave = (wave_ids == 0) | (wave_ids == half)
    weight = response * jnp.where(edge_wave, 1.0, 2.0) / circle
    return basis.T, weight[:, None] * basis


def filter_matrix(left_ref, right_ref, matrix_ref):
    block = matrix_ref.shape[0] // 4

    @pl.loop(0, 4)
    def _(i):
        rows = pl.ds(pl.multiple_of(i * block, block), block)
        matrix_ref[rows, :] = jnp.dot(
            left_ref[rows, :],
            right_ref[...],
            precision=HIGHEST,
            preferred_element_type=jnp.float32,
        )


def channel_columns(table_ref, coupling_ref, once_ref, twice_ref):
    def couple(value):
        return value + jnp.dot(
            value,
            coupling_ref[...],
            precision=HIGHEST,
            preferred_element_type=jnp.float32,
        )

    once = couple(table_ref[...])
    once_ref[...] = once
    twice_ref[...] = couple(once)


def row_neighbours(value, lon_groups, lat_groups):
    def device(row, part):
        return (row % LAT_DEV * PARTS + part) * lat_groups + row // LAT_DEV

    rows = LAT_DEV * lat_groups
    up = [(device(i, p), device(i + 1, p)) for i in range(rows - 1) for p in range(PARTS)]
    south = lax.ppermute(value, ("lon", "lat"), up)
    north = lax.ppermute(value, ("lon", "lat"), [(b, a) for a, b in up])
    return south, north


def per_device(
    zonal, merid, diffuse, coupling, table, obs_dep, obs_frac, obs_owner, obs_lon, obs_lat, obs_chan
):
    lon_groups = lax.axis_size("lon")
    lat_groups = lax.axis_size("lat")
    columns = FIELDS * LEV
    circle = LON_DEV * lon_groups
    lat_rows = LAT_DEV * lat_groups
    lat_index = lax.axis_index("lat")
    own_row = lat_index * LAT_DEV + lax.axis_index("lon") // PARTS
    factors = filter_factors(own_row, circle, lat_rows)

    steps, rows = obs_dep.shape
    dest_ids = jnp.arange(lon_groups, dtype=jnp.int32)
    chosen = (obs_owner == dest_ids).astype(jnp.float32)
    earlier = jnp.arange(rows)[:, None] > jnp.arange(rows)[None, :]
    before = lax.dot_general(
        jnp.broadcast_to(earlier.astype(jnp.float32), (steps, rows, rows)),
        chosen,
        (((2,), (1,)), ((0,), (0,))),
    )
    rank = jnp.sum(before * chosen, axis=2)[:, :, None]
    in_slot = rank == jnp.arange(CAP, dtype=jnp.float32)
    details = [
        obs_dep,
        obs_frac[:, :, 0],
        obs_frac[:, :, 1],
        obs_lon.astype(jnp.float32),
        obs_lat.astype(jnp.float32),
        obs_chan.astype(jnp.float32),
    ]
    slotted = jnp.concatenate([jnp.where(in_slot, d[:, :, None], 0.0) for d in details], axis=2)
    sent = lax.dot_general(chosen, slotted, (((1,), (1,)), ((0,), (0,))), precision=HIGHEST)
    by_row = [jnp.repeat(c.T, PARTS, axis=0) for c in (zonal, merid, diffuse)]
    spare = jnp.zeros((lon_groups, 8), jnp.float32)
    got, matrix = exchange(
        jnp.concatenate([sent[0], sent[1]] + by_row + [spare], axis=1),
        0,
        filter_matrix,
        factors,
        ((circle, circle),),
    )

    cells = jnp.arange(LAT_DEV * (LON_DEV + 1), dtype=jnp.int32)
    cell_lat = (cells // (LON_DEV + 1)).astype(jnp.float32)
    cell_lon = (cells % (LON_DEV + 1)).astype(jnp.float32)
    items = jnp.arange(PARTS * ITEMS, dtype=jnp.int32)
    item_step = items % ITEMS // SHARE
    item_chan = (items // ITEMS * SHARE + items % SHARE).astype(jnp.float32)
    weights, picks = [], []
    for step_id in range(steps):
        start = step_id * 6 * CAP
        dep, along, across, lon, lat, chan = (
            got[:, start + f * CAP : start + (f + 1) * CAP][:, :, None] for f in range(6)
        )
        lon_part = jnp.where(cell_lon == lon, 1.0 - along, 0.0)
        lon_part = lon_part + jnp.where(cell_lon == lon + 1.0, along, 0.0)
        lat_part = jnp.where(cell_lat == lat, 1.0 - across, 0.0)
        lat_part = lat_part + jnp.where(cell_lat == lat + 1.0, across, 0.0)
        weights.append((lon_part * lat_part).reshape(lon_groups * CAP, -1))
        hit = (item_chan == chan) & (item_step == step_id)
        picks.append(jnp.where(hit, dep, 0.0).reshape(lon_groups * CAP, -1))
    forcing = contract_first(jnp.concatenate(weights), jnp.concatenate(picks), HIGHEST)

    pieces = forcing.reshape(LAT_DEV, LON_DEV + 1, PARTS, ITEMS).transpose(0, 2, 1, 3)
    pieces = jnp.pad(pieces.reshape(lon_groups, -1), ((0, 0), (0, ITEMS)))
    pieces, once, twice = exchange(
        pieces,
        1,
        channel_columns,
        (table, coupling.T),
        (table.shape, table.shape),
    )
    edge = jnp.roll(pieces[:, LON_DEV * ITEMS : (LON_DEV + 1) * ITEMS], 1, axis=0)
    first = pieces[:, :ITEMS] + edge
    circles = jnp.concatenate([first, pieces[:, ITEMS : LON_DEV * ITEMS]], axis=1)
    circles = circles.reshape(circle, ITEMS)
    filtered = jnp.dot(matrix, circles, precision=HIGHEST)
    early, late = filtered[:, :SHARE], filtered[:, SHARE:]
    south, north = row_neighbours(late, lon_groups, lat_groups)
    first_coef = 12 * CAP
    own_zonal, own_merid, own_diffuse = (
        got[:, first_coef + n * LON_DEV : first_coef + (n + 1) * LON_DEV].reshape(circle, 1)
        for n in range(3)
    )
    moved = (1.0 - 4.0 * own_diffuse) * late
    moved = moved + (own_diffuse - 0.5 * own_zonal) * jnp.roll(late, 1, axis=0)
    moved = moved + (own_diffuse + 0.5 * own_zonal) * jnp.roll(late, -1, axis=0)
    moved = moved + (own_diffuse - 0.5 * own_merid) * south
    moved = moved + (own_diffuse + 0.5 * own_merid) * north
    again = jnp.dot(matrix, moved, precision=HIGHEST)

    both = jnp.concatenate([early, again], axis=1).reshape(lon_groups, LON_DEV * ITEMS)
    west = jnp.roll(both[:, (LON_DEV - 1) * ITEMS :], 1, axis=0)
    east = jnp.roll(both[:, :ITEMS], -1, axis=0)
    (back,) = exchange(jnp.concatenate([west, both, east], axis=1), 2)
    back = back.reshape(LAT_DEV, PARTS, LON_DEV + 2, ITEMS).transpose(2, 0, 1, 3)
    parts = (once.reshape(PARTS, SHARE, columns), twice.reshape(PARTS, SHARE, columns))
    columns_of = jnp.concatenate(parts, axis=1).reshape(PARTS * ITEMS, columns)
    cube = jnp.dot(
        back.reshape((LON_DEV + 2) * LAT_DEV, PARTS * ITEMS), columns_of, precision=HIGHEST
    ).reshape(LON_DEV + 2, LAT_DEV, columns)
    inner = cube[1:-1]
    up = [(i, i + 1) for i in range(lat_groups - 1)]
    south = lax.ppermute(inner[:, -1], "lat", up)
    north = lax.ppermute(inner[:, 0], "lat", [(b, a) for a, b in up])
    south = jnp.concatenate([south[:, None], inner[:, :-1]], axis=1)
    north = jnp.concatenate([inner[:, 1:], north[:, None]], axis=1)
    diffusion = diffuse[:, :, None]
    eastward = 0.5 * zonal[:, :, None]
    northward = 0.5 * merid[:, :, None]
    result = (1.0 - 4.0 * diffusion) * inner + (diffusion - eastward) * cube[:-2]
    result = result + (diffusion + eastward) * cube[2:]
    result = result + (diffusion - northward) * south
    result = result + (diffusion + northward) * north
    return result.reshape(LON_DEV, LAT_DEV * columns)


def solution(mesh):
    return jax.shard_map(
        per_device,
        mesh=mesh,
        in_specs=(
            P("lon", "lat"),
            P("lon", "lat"),
            P("lon", "lat"),
            P(),
            P(),
            P(None, ("lon", "lat")),
            P(None, ("lon", "lat"), None),
            P(None, ("lon", "lat"), None),
            P(None, ("lon", "lat")),
            P(None, ("lon", "lat")),
            P(None, ("lon", "lat")),
        ),
        out_specs=P("lon", "lat"),
        check_vma=False,
    )
```

```python
import functools
import math

import jax
import jax.numpy as jnp
import numpy as np
from jax import lax
from jax.experimental import pallas as pl
from jax.experimental.pallas import tpu as pltpu
from jax.sharding import PartitionSpec as P

FIELDS = 5
LEV = 72
NCHAN = 128
LON_DEV = 8
LAT_DEV = 16
CAP = 8
PARTS = 4
SHARE = NCHAN // PARTS
ITEMS = 2 * SHARE


HALF_ROOT = 0.7071067811865476
HIGHEST = lax.Precision.HIGHEST


def contract_first(left, right, precision):
    return lax.dot_general(left, right, (((0,), (0,)), ((), ())), precision=precision)


def exchange_kernel(compute, reads, edges, *refs):
    sent, extra, got = refs[0], refs[1 : 1 + reads], refs[1 + reads]
    made, (mid, *sems) = refs[2 + reads : -len(SEMS) - 1], refs[-len(SEMS) - 1 :]
    near_send, near_recv, far_send, far_recv, own_sem, edge_send, edge_recv = sems
    groups, members = sent.shape[:2]
    me, lat = lax.axis_index("lon"), lax.axis_index("lat")
    group, member = me // members, lax.rem(me, members)
    lat_groups = lax.axis_size("lat")

    def in_group(shift):
        place = lax.rem(member + shift, members)
        return place, {"lon": group * members + place}

    def across(shift):
        place = lax.rem(group + shift, groups)
        return place, {"lon": place * members + member}

    beside = [{"lat": lax.rem(lat + shift, lat_groups)} for shift in (1, lat_groups - 1)]
    barrier = pltpu.get_barrier_semaphore()

    def greet(device):
        pl.semaphore_signal(
            barrier, inc=1, device_id=device, device_id_type=pl.DeviceIdType.MESH
        )

    def remote(source, target, send_sem, recv_sem, device):
        return pltpu.make_async_remote_copy(
            src_ref=source,
            dst_ref=target,
            send_sem=send_sem,
            recv_sem=recv_sem,
            device_id=device,
            device_id_type=pl.DeviceIdType.MESH,
        )

    @pl.loop(1, members)
    def _(shift):
        greet(in_group(shift)[1])

    @pl.loop(1, groups)
    def _(shift):
        greet(across(shift)[1])

    if edges:
        for device in beside:
            greet(device)
    own = pltpu.make_async_copy(sent.at[:, member], mid.at[member], own_sem)
    own.start()
    pl.semaphore_wait(barrier, members + groups - 2 + (2 if edges else 0))

    @pl.loop(1, members)
    def _(shift):
        place, device = in_group(shift)
        remote(sent.at[:, place], mid.at[member], near_send, near_recv, device).start()

    if compute is not None:
        compute(*extra, *made)
    own.wait()
    rest = mid.at[pl.ds(0, members - 1)]
    remote(rest, rest, near_send, near_recv, in_group(1)[1]).wait()

    own = pltpu.make_async_copy(mid.at[:, group], got.at[group], own_sem)
    own.start()

    @pl.loop(1, groups)
    def _(shift):
        place, device = across(shift)
        remote(mid.at[:, place], got.at[group], far_send, far_recv, device).start()

    own.wait()
    rest = got.at[pl.ds(0, groups - 1)]
    remote(rest, rest, far_send, far_recv, across(1)[1]).wait()
    if edges:
        rows = made[-1]
        last = got.at[groups - 1, pl.ds(members - PARTS, PARTS)]
        first = got.at[0, pl.ds(0, PARTS)]
        north = remote(last, rows.at[0], edge_send.at[0], edge_recv.at[0], beside[0])
        south = remote(first, rows.at[1], edge_send.at[1], edge_recv.at[1], beside[1])
        north.start()
        south.start()
        north.wait()
        south.wait()


SEMS = (None, None, None, None, None, (2,), (2,))
GROUPS = 4


def exchange(value, number, compute=None, extra=(), made=(), edges=False):
    count, width = value.shape
    members = count // GROUPS
    if edges:
        made = tuple(made) + ((2, PARTS, 1, width),)
    shape = (GROUPS, members, 1, width)
    in_vmem = pl.BlockSpec(memory_space=pltpu.VMEM)
    dma = pltpu.SemaphoreType.DMA
    outs = pl.pallas_call(
        functools.partial(exchange_kernel, compute, len(extra), edges),
        out_shape=tuple(jax.ShapeDtypeStruct(m, jnp.float32) for m in (shape,) + tuple(made)),
        in_specs=[in_vmem] * (1 + len(extra)),
        out_specs=(in_vmem,) * (1 + len(made)),
        scratch_shapes=[pltpu.VMEM((members, GROUPS, 1, width), jnp.float32)]
        + [dma if s is None else dma(s) for s in SEMS],
        compiler_params=pltpu.CompilerParams(collective_id=number, has_side_effects=True),
    )(value.reshape(shape), *extra)
    return (outs[0].reshape(count, width),) + tuple(outs[1:])


def filter_factors(row, circle, lat_rows):
    half = circle // 2
    waves = np.concatenate([np.arange(half + 1), np.arange(1, half)])
    phase = waves[:, None] * np.arange(circle)[None, :] % circle * (2.0 * math.pi / circle)
    basis = np.where(np.arange(circle)[:, None] <= half, np.cos(phase), np.sin(phase))
    basis = basis.astype(np.float32)
    coslat = jnp.cos((row.astype(jnp.float32) + 0.5) * (math.pi / lat_rows) - 0.5 * math.pi)
    sines = np.sin(waves * (math.pi / circle)).astype(np.float32)
    response = coslat / jnp.maximum(HALF_ROOT * sines, coslat)
    inverse = np.where((waves == 0) | (waves == half), 1.0, 2.0).astype(np.float32) / circle
    return jnp.asarray(basis.T), jnp.asarray(basis), (response * inverse)[None, :]


def filter_matrix(left_ref, right_ref, weight_ref, matrix_ref):
    block = matrix_ref.shape[0] // 4

    @pl.loop(0, 4)
    def _(i):
        rows = pl.ds(pl.multiple_of(i * block, block), block)
        matrix_ref[rows, :] = jnp.dot(
            left_ref[rows, :] * weight_ref[...],
            right_ref[...],
            precision=HIGHEST,
            preferred_element_type=jnp.float32,
        )


def channel_columns(table_ref, coupling_ref, once_ref, twice_ref):
    def couple(value):
        return value + jnp.dot(
            value,
            coupling_ref[...],
            precision=HIGHEST,
            preferred_element_type=jnp.float32,
        )

    once = couple(table_ref[...])
    once_ref[...] = once
    twice_ref[...] = couple(once)


def row_neighbours(value, lon_groups, lat_groups):
    def device(row, part):
        return (row % LAT_DEV * PARTS + part) * lat_groups + row // LAT_DEV

    rows = LAT_DEV * lat_groups
    up = [(device(i, p), device(i + 1, p)) for i in range(rows - 1) for p in range(PARTS)]
    south = lax.ppermute(value, ("lon", "lat"), up)
    north = lax.ppermute(value, ("lon", "lat"), [(b, a) for a, b in up])
    return south, north


def per_device(
    zonal, merid, diffuse, coupling, table, obs_dep, obs_frac, obs_owner, obs_lon, obs_lat, obs_chan
):
    lon_groups = lax.axis_size("lon")
    lat_groups = lax.axis_size("lat")
    columns = FIELDS * LEV
    circle = LON_DEV * lon_groups
    lat_rows = LAT_DEV * lat_groups
    lat_index = lax.axis_index("lat")
    own_row = lat_index * LAT_DEV + lax.axis_index("lon") // PARTS
    factors = filter_factors(own_row, circle, lat_rows)

    steps, rows = obs_dep.shape
    dest_ids = jnp.arange(lon_groups, dtype=jnp.int32)
    chosen = (obs_owner == dest_ids).astype(jnp.float32)
    earlier = jnp.arange(rows)[:, None] > jnp.arange(rows)[None, :]
    before = lax.dot_general(
        jnp.broadcast_to(earlier.astype(jnp.float32), (steps, rows, rows)),
        chosen,
        (((2,), (1,)), ((0,), (0,))),
    )
    rank = jnp.sum(before * chosen, axis=2)[:, :, None]
    in_slot = rank == jnp.arange(CAP, dtype=jnp.float32)
    details = [
        obs_dep,
        obs_frac[:, :, 0],
        obs_frac[:, :, 1],
        obs_lon.astype(jnp.float32),
        obs_lat.astype(jnp.float32),
        obs_chan.astype(jnp.float32),
    ]
    slotted = jnp.concatenate([jnp.where(in_slot, d[:, :, None], 0.0) for d in details], axis=2)
    sent = lax.dot_general(chosen, slotted, (((1,), (1,)), ((0,), (0,))), precision=HIGHEST)
    by_row = [jnp.repeat(c.T, PARTS, axis=0) for c in (zonal, merid, diffuse)]
    spare = jnp.zeros((lon_groups, 8), jnp.float32)
    got, matrix = exchange(
        jnp.concatenate([sent[0], sent[1]] + by_row + [spare], axis=1),
        0,
        filter_matrix,
        factors,
        ((circle, circle),),
    )

    cells = jnp.arange(LAT_DEV * (LON_DEV + 1), dtype=jnp.int32)
    cell_lat = (cells // (LON_DEV + 1)).astype(jnp.float32)
    cell_lon = (cells % (LON_DEV + 1)).astype(jnp.float32)
    items = jnp.arange(PARTS * ITEMS, dtype=jnp.int32)
    item_step = items % ITEMS // SHARE
    item_chan = (items // ITEMS * SHARE + items % SHARE).astype(jnp.float32)
    weights, picks = [], []
    for step_id in range(steps):
        start = step_id * 6 * CAP
        dep, along, across, lon, lat, chan = (
            got[:, start + f * CAP : start + (f + 1) * CAP][:, :, None] for f in range(6)
        )
        lon_part = jnp.where(cell_lon == lon, 1.0 - along, 0.0)
        lon_part = lon_part + jnp.where(cell_lon == lon + 1.0, along, 0.0)
        lat_part = jnp.where(cell_lat == lat, 1.0 - across, 0.0)
        lat_part = lat_part + jnp.where(cell_lat == lat + 1.0, across, 0.0)
        weights.append((lon_part * lat_part).reshape(lon_groups * CAP, -1))
        hit = (item_chan == chan) & (item_step == step_id)
        picks.append(jnp.where(hit, dep, 0.0).reshape(lon_groups * CAP, -1))
    forcing = contract_first(jnp.concatenate(weights), jnp.concatenate(picks), HIGHEST)

    pieces = forcing.reshape(LAT_DEV, LON_DEV + 1, PARTS, ITEMS).transpose(0, 2, 1, 3)
    pieces = jnp.pad(pieces.reshape(lon_groups, -1), ((0, 0), (0, ITEMS)))
    pieces, once, twice = exchange(
        pieces,
        1,
        channel_columns,
        (table, coupling.T),
        (table.shape, table.shape),
    )
    edge = jnp.roll(pieces[:, LON_DEV * ITEMS : (LON_DEV + 1) * ITEMS], 1, axis=0)
    first = pieces[:, :ITEMS] + edge
    circles = jnp.concatenate([first, pieces[:, ITEMS : LON_DEV * ITEMS]], axis=1)
    circles = circles.reshape(circle, ITEMS)
    filtered = jnp.dot(matrix, circles, precision=HIGHEST)
    early, late = filtered[:, :SHARE], filtered[:, SHARE:]
    south, north = row_neighbours(late, lon_groups, lat_groups)
    first_coef = 12 * CAP
    own_zonal, own_merid, own_diffuse = (
        got[:, first_coef + n * LON_DEV : first_coef + (n + 1) * LON_DEV].reshape(circle, 1)
        for n in range(3)
    )
    moved = (1.0 - 4.0 * own_diffuse) * late
    moved = moved + (own_diffuse - 0.5 * own_zonal) * jnp.roll(late, 1, axis=0)
    moved = moved + (own_diffuse + 0.5 * own_zonal) * jnp.roll(late, -1, axis=0)
    moved = moved + (own_diffuse - 0.5 * own_merid) * south
    moved = moved + (own_diffuse + 0.5 * own_merid) * north
    again = jnp.dot(matrix, moved, precision=HIGHEST)

    both = jnp.concatenate([early, again], axis=1).reshape(lon_groups, LON_DEV * ITEMS)
    west = jnp.roll(both[:, (LON_DEV - 1) * ITEMS :], 1, axis=0)
    east = jnp.roll(both[:, :ITEMS], -1, axis=0)
    back, beside = exchange(jnp.concatenate([west, both, east], axis=1), 2, edges=True)
    inside = jnp.array([lat_index > 0, lat_index < lat_groups - 1])[:, None, None]
    beside = jnp.where(inside, beside.reshape(2, PARTS, -1), 0.0)
    back = jnp.concatenate([beside[0], back, beside[1]], axis=0)
    back = back.reshape(LAT_DEV + 2, PARTS, LON_DEV + 2, ITEMS).transpose(2, 0, 1, 3)
    parts = (once.reshape(PARTS, SHARE, columns), twice.reshape(PARTS, SHARE, columns))
    columns_of = jnp.concatenate(parts, axis=1).reshape(PARTS * ITEMS, columns)
    cube = jnp.dot(
        back.reshape((LON_DEV + 2) * (LAT_DEV + 2), PARTS * ITEMS), columns_of, precision=HIGHEST
    ).reshape(LON_DEV + 2, LAT_DEV + 2, columns)
    diffusion = diffuse[:, :, None]
    eastward = 0.5 * zonal[:, :, None]
    northward = 0.5 * merid[:, :, None]
    result = (1.0 - 4.0 * diffusion) * cube[1:-1, 1:-1]
    result = result + (diffusion - eastward) * cube[:-2, 1:-1]
    result = result + (diffusion + eastward) * cube[2:, 1:-1]
    result = result + (diffusion - northward) * cube[1:-1, :-2]
    result = result + (diffusion + northward) * cube[1:-1, 2:]
    return result.reshape(LON_DEV, LAT_DEV * columns)


def solution(mesh):
    return jax.shard_map(
        per_device,
        mesh=mesh,
        in_specs=(
            P("lon", "lat"),
            P("lon", "lat"),
            P("lon", "lat"),
            P(),
            P(),
            P(None, ("lon", "lat")),
            P(None, ("lon", "lat"), None),
            P(None, ("lon", "lat"), None),
            P(None, ("lon", "lat")),
            P(None, ("lon", "lat")),
            P(None, ("lon", "lat")),
        ),
        out_specs=P("lon", "lat"),
        check_vma=False,
    )
```

```python
import functools
import math

import jax
import jax.numpy as jnp
import numpy as np
from jax import lax
from jax.experimental import pallas as pl
from jax.experimental.pallas import tpu as pltpu
from jax.sharding import PartitionSpec as P

FIELDS = 5
LEV = 72
NCHAN = 128
LON_DEV = 8
LAT_DEV = 16
CAP = 8
PARTS = 4
SHARE = NCHAN // PARTS
ITEMS = 2 * SHARE


HALF_ROOT = 0.7071067811865476
HIGHEST = lax.Precision.HIGHEST


def contract_first(left, right, precision):
    return lax.dot_general(left, right, (((0,), (0,)), ((), ())), precision=precision)


def remote(source, target, send_sem, recv_sem, device):
    return pltpu.make_async_remote_copy(
        src_ref=source,
        dst_ref=target,
        send_sem=send_sem,
        recv_sem=recv_sem,
        device_id=device,
        device_id_type=pl.DeviceIdType.MESH,
    )


def greet(device):
    pl.semaphore_signal(
        pltpu.get_barrier_semaphore(),
        inc=1,
        device_id=device,
        device_id_type=pl.DeviceIdType.MESH,
    )


def in_group(shift, members):
    me = lax.axis_index("lon")
    place = lax.rem(lax.rem(me, members) + shift, members)
    return place, {"lon": me // members * members + place}


def across(shift, groups, members):
    me = lax.axis_index("lon")
    place = lax.rem(me // members + shift, groups)
    return place, {"lon": place * members + lax.rem(me, members)}


def greet_all(groups, members, more=()):
    @pl.loop(1, members)
    def _(shift):
        greet(in_group(shift, members)[1])

    @pl.loop(1, groups)
    def _(shift):
        greet(across(shift, groups, members)[1])

    for device in more:
        greet(device)
    pl.semaphore_wait(pltpu.get_barrier_semaphore(), members + groups - 2 + len(more))


def two_phases(sent, mid, got, sems, compute=None):
    near_send, near_recv, far_send, far_recv, own_sem = (sems.at[i] for i in range(5))
    groups, members = sent.shape[:2]
    me = lax.axis_index("lon")
    group, member = me // members, lax.rem(me, members)
    own = pltpu.make_async_copy(sent.at[:, member], mid.at[member], own_sem)
    own.start()

    @pl.loop(1, members)
    def _(shift):
        place, device = in_group(shift, members)
        remote(sent.at[:, place], mid.at[member], near_send, near_recv, device).start()

    if compute is not None:
        compute()
    own.wait()
    rest = mid.at[pl.ds(0, members - 1)]
    remote(rest, rest, near_send, near_recv, in_group(1, members)[1]).wait()

    own = pltpu.make_async_copy(mid.at[:, group], got.at[group], own_sem)
    own.start()

    @pl.loop(1, groups)
    def _(shift):
        place, device = across(shift, groups, members)
        remote(mid.at[:, place], got.at[group], far_send, far_recv, device).start()

    own.wait()
    rest = got.at[pl.ds(0, groups - 1)]
    remote(rest, rest, far_send, far_recv, across(1, groups, members)[1]).wait()


def both_ways(up, down, landed, sems, above, below):
    first = remote(up, landed.at[0], sems.at[0], sems.at[1], above)
    second = remote(down, landed.at[1], sems.at[2], sems.at[3], below)
    first.start()
    second.start()
    first.wait()
    second.wait()


def product(left, right):
    return jnp.dot(left, right, precision=HIGHEST, preferred_element_type=jnp.float32)


def details_kernel(sent, left, right, weight, got, matrix, mid, sems):
    greet_all(*sent.shape[:2])
    two_phases(sent, mid, got, sems, lambda: filter_matrix(left, right, weight, matrix))


def steps_kernel(
    sent,
    matrix,
    coefs,
    table,
    coupling,
    back,
    beside,
    once,
    twice,
    mid,
    got,
    late_rows,
    late_beside,
    resent,
    mid_back,
    sems,
    back_sems,
    late_sems,
    edge_sems,
):
    groups, members = sent.shape[:2]
    count = groups * members
    me, lat = lax.axis_index("lon"), lax.axis_index("lat")
    lat_groups = lax.axis_size("lat")
    bands = [{"lat": lax.rem(lat + shift, lat_groups)} for shift in (1, lat_groups - 1)]
    own_row = lat * LAT_DEV + me // PARTS
    lat_rows = lat_groups * LAT_DEV
    rows = [lax.rem(own_row + shift, lat_rows) for shift in (1, lat_rows - 1)]
    rows = [
        {"lon": lax.rem(row, LAT_DEV) * PARTS + lax.rem(me, PARTS), "lat": row // LAT_DEV}
        for row in rows
    ]
    greet_all(groups, members, bands + rows)
    two_phases(sent, mid, got, sems, lambda: channel_columns(table, coupling, once, twice))

    def blocks(value):
        return [value[i * count : (i + 1) * count] for i in range(LON_DEV)]

    def shifted(value, forward):
        if forward:
            return jnp.concatenate([value[-1:], value[:-1]], axis=0)
        return jnp.concatenate([value[1:], value[:1]], axis=0)

    pieces = got[...].reshape(count, got.shape[3])
    circles = [pieces[:, i * ITEMS : (i + 1) * ITEMS] for i in range(LON_DEV + 1)]
    circles[0] = circles[0] + shifted(circles.pop(), True)
    filtered = product(matrix[...], jnp.concatenate(circles, axis=0))
    early, late = filtered[:, :SHARE], filtered[:, SHARE:]
    quarter = late.shape[0] // 4
    late_rows[...] = jnp.concatenate(
        [late[i * quarter : (i + 1) * quarter] for i in range(4)], axis=1
    )
    both_ways(late_rows, late_rows, late_beside, late_sems, *rows)

    def unpacked(value):
        return jnp.concatenate([value[:, i * SHARE : (i + 1) * SHARE] for i in range(4)], axis=0)

    parts = blocks(late)
    west = jnp.concatenate([shifted(parts[-1], True)] + parts[:-1], axis=0)
    east = jnp.concatenate(parts[1:] + [shifted(parts[0], False)], axis=0)
    sides = [late, west, east, unpacked(late_beside[0]), unpacked(late_beside[1])]
    moved = coefs[:, 0:1] * sides[0]
    for i in range(1, 5):
        moved = moved + coefs[:, i : i + 1] * sides[i]
    again = product(matrix[...], moved)
    parts = blocks(jnp.concatenate([early, again], axis=1))
    wide = [shifted(parts[-1], True)] + parts + [shifted(parts[0], False)]
    resent[...] = jnp.concatenate(wide, axis=1).reshape(resent.shape)
    two_phases(resent, mid_back, back, back_sems)
    last = back.at[groups - 1, pl.ds(members - PARTS, PARTS)]
    both_ways(last, back.at[0, pl.ds(0, PARTS)], beside, edge_sems, *bands)


GROUPS = 4


def call(kernel, number, outs, scratch, sems, *args):
    in_vmem = pl.BlockSpec(memory_space=pltpu.VMEM)
    return pl.pallas_call(
        kernel,
        out_shape=tuple(jax.ShapeDtypeStruct(shape, jnp.float32) for shape in outs),
        in_specs=[in_vmem] * len(args),
        out_specs=(in_vmem,) * len(outs),
        scratch_shapes=[pltpu.VMEM(shape, jnp.float32) for shape in scratch]
        + [pltpu.SemaphoreType.DMA((n,)) for n in sems],
        compiler_params=pltpu.CompilerParams(
            collective_id=number, has_side_effects=True, vmem_limit_bytes=48 * 1024 * 1024
        ),
    )(*args)


def by_groups(value):
    count, width = value.shape
    return value.reshape(GROUPS, count // GROUPS, 1, width)


def filter_factors(row, circle, lat_rows):
    half = circle // 2
    waves = np.concatenate([np.arange(half + 1), np.arange(1, half)])
    cells = np.arange(circle).reshape(-1, LON_DEV).T.reshape(1, circle)
    phase = waves[:, None] * cells % circle * (2.0 * math.pi / circle)
    basis = np.where(np.arange(circle)[:, None] <= half, np.cos(phase), np.sin(phase))
    basis = basis.astype(np.float32)
    coslat = jnp.cos((row.astype(jnp.float32) + 0.5) * (math.pi / lat_rows) - 0.5 * math.pi)
    sines = np.sin(waves * (math.pi / circle)).astype(np.float32)
    response = coslat / jnp.maximum(HALF_ROOT * sines, coslat)
    inverse = np.where((waves == 0) | (waves == half), 1.0, 2.0).astype(np.float32) / circle
    return jnp.asarray(basis.T), jnp.asarray(basis), (response * inverse)[None, :]


def filter_matrix(left_ref, right_ref, weight_ref, matrix_ref):
    block = matrix_ref.shape[0] // 4

    @pl.loop(0, 4)
    def _(i):
        rows = pl.ds(pl.multiple_of(i * block, block), block)
        matrix_ref[rows, :] = jnp.dot(
            left_ref[rows, :] * weight_ref[...],
            right_ref[...],
            precision=HIGHEST,
            preferred_element_type=jnp.float32,
        )


def channel_columns(table_ref, coupling_ref, once_ref, twice_ref):
    def couple(value):
        return value + jnp.dot(
            value,
            coupling_ref[...],
            precision=HIGHEST,
            preferred_element_type=jnp.float32,
        )

    once = couple(table_ref[...])
    once_ref[...] = once
    twice_ref[...] = couple(once)


def per_device(
    zonal, merid, diffuse, coupling, table, obs_dep, obs_frac, obs_owner, obs_lon, obs_lat, obs_chan
):
    lon_groups = lax.axis_size("lon")
    lat_groups = lax.axis_size("lat")
    columns = FIELDS * LEV
    circle = LON_DEV * lon_groups
    lat_rows = LAT_DEV * lat_groups
    lat_index = lax.axis_index("lat")
    own_row = lat_index * LAT_DEV + lax.axis_index("lon") // PARTS
    factors = filter_factors(own_row, circle, lat_rows)

    steps, rows = obs_dep.shape
    dest_ids = jnp.arange(lon_groups, dtype=jnp.int32)
    chosen = (obs_owner == dest_ids).astype(jnp.float32)
    earlier = jnp.arange(rows)[:, None] > jnp.arange(rows)[None, :]
    before = lax.dot_general(
        jnp.broadcast_to(earlier.astype(jnp.float32), (steps, rows, rows)),
        chosen,
        (((2,), (1,)), ((0,), (0,))),
    )
    rank = jnp.sum(before * chosen, axis=2)[:, :, None]
    in_slot = rank == jnp.arange(CAP, dtype=jnp.float32)
    details = [
        obs_dep,
        obs_frac[:, :, 0],
        obs_frac[:, :, 1],
        obs_lon.astype(jnp.float32),
        obs_lat.astype(jnp.float32),
        obs_chan.astype(jnp.float32),
    ]
    slotted = jnp.concatenate([jnp.where(in_slot, d[:, :, None], 0.0) for d in details], axis=2)
    sent = lax.dot_general(chosen, slotted, (((1,), (1,)), ((0,), (0,))), precision=HIGHEST)
    by_row = [jnp.repeat(c.T, PARTS, axis=0) for c in (zonal, merid, diffuse)]
    spare = jnp.zeros((lon_groups, 8), jnp.float32)
    sent = by_groups(jnp.concatenate([sent[0], sent[1]] + by_row + [spare], axis=1))
    turned = (sent.shape[1], sent.shape[0]) + sent.shape[2:]
    got, matrix = call(
        details_kernel, 0, (sent.shape, (circle, circle)), (turned,), (5,), sent, *factors
    )
    got = got.reshape(lon_groups, -1)

    cells = jnp.arange(LAT_DEV * (LON_DEV + 1), dtype=jnp.int32)
    cell_lat = (cells // (LON_DEV + 1)).astype(jnp.float32)
    cell_lon = (cells % (LON_DEV + 1)).astype(jnp.float32)
    items = jnp.arange(PARTS * ITEMS, dtype=jnp.int32)
    item_step = items % ITEMS // SHARE
    item_chan = (items // ITEMS * SHARE + items % SHARE).astype(jnp.float32)
    weights, picks = [], []
    for step_id in range(steps):
        start = step_id * 6 * CAP
        dep, along, across, lon, lat, chan = (
            got[:, start + f * CAP : start + (f + 1) * CAP][:, :, None] for f in range(6)
        )
        lon_part = jnp.where(cell_lon == lon, 1.0 - along, 0.0)
        lon_part = lon_part + jnp.where(cell_lon == lon + 1.0, along, 0.0)
        lat_part = jnp.where(cell_lat == lat, 1.0 - across, 0.0)
        lat_part = lat_part + jnp.where(cell_lat == lat + 1.0, across, 0.0)
        weights.append((lon_part * lat_part).reshape(lon_groups * CAP, -1))
        hit = (item_chan == chan) & (item_step == step_id)
        picks.append(jnp.where(hit, dep, 0.0).reshape(lon_groups * CAP, -1))
    forcing = contract_first(jnp.concatenate(weights), jnp.concatenate(picks), HIGHEST)

    pieces = forcing.reshape(LAT_DEV, LON_DEV + 1, PARTS, ITEMS).transpose(0, 2, 1, 3)
    pieces = by_groups(jnp.pad(pieces.reshape(lon_groups, -1), ((0, 0), (0, ITEMS))))
    first_coef = 12 * CAP
    own_zonal, own_merid, own_diffuse = (
        got[:, first_coef + n * LON_DEV : first_coef + (n + 1) * LON_DEV].T.reshape(circle)
        for n in range(3)
    )
    own_row = jnp.full((circle,), own_row)
    coefs = [
        1.0 - 4.0 * own_diffuse,
        own_diffuse - 0.5 * own_zonal,
        own_diffuse + 0.5 * own_zonal,
        jnp.where(own_row > 0, own_diffuse - 0.5 * own_merid, 0.0),
        jnp.where(own_row < lat_rows - 1, own_diffuse + 0.5 * own_merid, 0.0),
    ]

    packed = (circle // 4, 4 * SHARE)
    turned = (pieces.shape[1], pieces.shape[0]) + pieces.shape[2:]
    back, beside, once, twice = call(
        steps_kernel,
        1,
        (pieces.shape, (2, PARTS) + pieces.shape[2:], table.shape, table.shape),
        (turned, pieces.shape, packed, (2,) + packed, pieces.shape, turned),
        (5, 5, 4, 4),
        pieces,
        matrix,
        jnp.stack(coefs, axis=1),
        table,
        coupling.T,
    )
    back = back.reshape(lon_groups, -1)
    inside = jnp.array([lat_index > 0, lat_index < lat_groups - 1])[:, None, None]
    beside = jnp.where(inside, beside.reshape(2, PARTS, -1), 0.0)
    back = jnp.concatenate([beside[0], back, beside[1]], axis=0)
    back = back.reshape(LAT_DEV + 2, PARTS, LON_DEV + 2, ITEMS).transpose(2, 0, 1, 3)
    parts = (once.reshape(PARTS, SHARE, columns), twice.reshape(PARTS, SHARE, columns))
    columns_of = jnp.concatenate(parts, axis=1).reshape(PARTS * ITEMS, columns)
    cube = jnp.dot(
        back.reshape((LON_DEV + 2) * (LAT_DEV + 2), PARTS * ITEMS), columns_of, precision=HIGHEST
    ).reshape(LON_DEV + 2, LAT_DEV + 2, columns)
    diffusion = diffuse[:, :, None]
    eastward = 0.5 * zonal[:, :, None]
    northward = 0.5 * merid[:, :, None]
    result = (1.0 - 4.0 * diffusion) * cube[1:-1, 1:-1]
    result = result + (diffusion - eastward) * cube[:-2, 1:-1]
    result = result + (diffusion + eastward) * cube[2:, 1:-1]
    result = result + (diffusion - northward) * cube[1:-1, :-2]
    result = result + (diffusion + northward) * cube[1:-1, 2:]
    return result.reshape(LON_DEV, LAT_DEV * columns)


def solution(mesh):
    return jax.shard_map(
        per_device,
        mesh=mesh,
        in_specs=(
            P("lon", "lat"),
            P("lon", "lat"),
            P("lon", "lat"),
            P(),
            P(),
            P(None, ("lon", "lat")),
            P(None, ("lon", "lat"), None),
            P(None, ("lon", "lat"), None),
            P(None, ("lon", "lat")),
            P(None, ("lon", "lat")),
            P(None, ("lon", "lat")),
        ),
        out_specs=P("lon", "lat"),
        check_vma=False,
    )
```

```python
import functools
import math

import jax
import jax.numpy as jnp
import numpy as np
from jax import lax
from jax.experimental import pallas as pl
from jax.experimental.pallas import tpu as pltpu
from jax.sharding import PartitionSpec as P

FIELDS = 5
LEV = 72
NCHAN = 128
LON_DEV = 8
LAT_DEV = 16
CAP = 8
PARTS = 4
SHARE = NCHAN // PARTS
ITEMS = 2 * SHARE


HALF_ROOT = 0.7071067811865476
HIGHEST = lax.Precision.HIGHEST


def contract_first(left, right, precision):
    return lax.dot_general(left, right, (((0,), (0,)), ((), ())), precision=precision)


def remote(source, target, send_sem, recv_sem, device):
    return pltpu.make_async_remote_copy(
        src_ref=source,
        dst_ref=target,
        send_sem=send_sem,
        recv_sem=recv_sem,
        device_id=device,
        device_id_type=pl.DeviceIdType.MESH,
    )


def greet(device):
    pl.semaphore_signal(
        pltpu.get_barrier_semaphore(),
        inc=1,
        device_id=device,
        device_id_type=pl.DeviceIdType.MESH,
    )


def in_group(shift, members):
    me = lax.axis_index("lon")
    place = lax.rem(lax.rem(me, members) + shift, members)
    return place, {"lon": me // members * members + place}


def across(shift, groups, members):
    me = lax.axis_index("lon")
    place = lax.rem(me // members + shift, groups)
    return place, {"lon": place * members + lax.rem(me, members)}


def greet_all(groups, members, more=()):
    @pl.loop(1, members)
    def _(shift):
        greet(in_group(shift, members)[1])

    @pl.loop(1, groups)
    def _(shift):
        greet(across(shift, groups, members)[1])

    for device in more:
        greet(device)
    pl.semaphore_wait(pltpu.get_barrier_semaphore(), members + groups - 2 + len(more))


def two_phases(sent, mid, got, sems, compute=None):
    near_send, near_recv, far_send, far_recv, own_sem = (sems.at[i] for i in range(5))
    groups, members = sent.shape[:2]
    me = lax.axis_index("lon")
    group, member = me // members, lax.rem(me, members)
    own = pltpu.make_async_copy(sent.at[:, member], mid.at[member], own_sem)
    own.start()

    @pl.loop(1, members)
    def _(shift):
        place, device = in_group(shift, members)
        remote(sent.at[:, place], mid.at[member], near_send, near_recv, device).start()

    if compute is not None:
        compute()
    own.wait()
    rest = mid.at[pl.ds(0, members - 1)]
    remote(rest, rest, near_send, near_recv, in_group(1, members)[1]).wait()

    own = pltpu.make_async_copy(mid.at[:, group], got.at[group], own_sem)
    own.start()

    @pl.loop(1, groups)
    def _(shift):
        place, device = across(shift, groups, members)
        remote(mid.at[:, place], got.at[group], far_send, far_recv, device).start()

    own.wait()
    rest = got.at[pl.ds(0, groups - 1)]
    remote(rest, rest, far_send, far_recv, across(1, groups, members)[1]).wait()


def peer(shift):
    count = lax.axis_size("lon")
    return lax.rem(lax.axis_index("lon") + shift, count)


def start_direct(sent, got, sems):
    me, count = lax.axis_index("lon"), lax.axis_size("lon")
    own = pltpu.make_async_copy(sent.at[me], got.at[me], sems.at[2])
    own.start()

    @pl.loop(1, count)
    def _(shift):
        place = peer(shift)
        remote(sent.at[place], got.at[me], sems.at[0], sems.at[1], {"lon": place}).start()

    def finish():
        own.wait()
        rest = got.at[pl.ds(0, count - 1)]
        remote(rest, rest, sems.at[0], sems.at[1], {"lon": peer(1)}).wait()

    return finish


def both_ways(up, down, landed, sems, above, below):
    first = remote(up, landed.at[0], sems.at[0], sems.at[1], above)
    second = remote(down, landed.at[1], sems.at[2], sems.at[3], below)
    first.start()
    second.start()

    def finish():
        first.wait()
        second.wait()

    return finish


def product(left, right):
    return jnp.dot(left, right, precision=HIGHEST, preferred_element_type=jnp.float32)


def details_kernel(sent, left, right, weight, got, matrix, mid, sems):
    greet_all(*sent.shape[:2])
    two_phases(sent, mid, got, sems, lambda: filter_matrix(left, right, weight, matrix))


def steps_kernel(
    sent_early,
    sent_late,
    matrix,
    coefs,
    table,
    coupling,
    back_early,
    back_late,
    beside_early,
    beside_late,
    once,
    twice,
    got_early,
    got_late,
    late_rows,
    late_beside,
    resent_early,
    resent_late,
    *sems,
):
    count = sent_early.shape[0]
    me, lat = lax.axis_index("lon"), lax.axis_index("lat")
    lat_groups = lax.axis_size("lat")
    bands = [{"lat": lax.rem(lat + shift, lat_groups)} for shift in (1, lat_groups - 1)]
    own_row = lat * LAT_DEV + me // PARTS
    lat_rows = lat_groups * LAT_DEV
    rows = [lax.rem(own_row + shift, lat_rows) for shift in (1, lat_rows - 1)]
    rows = [
        {"lon": lax.rem(row, LAT_DEV) * PARTS + lax.rem(me, PARTS), "lat": row // LAT_DEV}
        for row in rows
    ]

    @pl.loop(1, count)
    def _(shift):
        greet({"lon": peer(shift)})

    for device in bands + rows:
        greet(device)
    channel_columns(table, coupling, once, twice)
    pl.semaphore_wait(pltpu.get_barrier_semaphore(), count + 3)
    late_came = start_direct(sent_late, got_late, sems[0])
    early_came = start_direct(sent_early, got_early, sems[1])

    def blocks(value):
        return [value[i * count : (i + 1) * count] for i in range(LON_DEV)]

    def shifted(value, forward):
        if forward:
            return jnp.concatenate([value[-1:], value[:-1]], axis=0)
        return jnp.concatenate([value[1:], value[:1]], axis=0)

    def filtered(got):
        pieces = got[...].reshape(count, got.shape[2])
        circles = [pieces[:, i * SHARE : (i + 1) * SHARE] for i in range(LON_DEV + 1)]
        circles[0] = circles[0] + shifted(circles.pop(), True)
        return product(matrix[...], jnp.concatenate(circles, axis=0))

    def send_back(value, resent, back, back_sems):
        parts = blocks(value)
        wide = [shifted(parts[-1], True)] + parts + [shifted(parts[0], False)]
        wide = wide + [jnp.zeros_like(parts[0])] * (resent.shape[2] // SHARE - len(wide))
        resent[...] = jnp.concatenate(wide, axis=1).reshape(resent.shape)
        return start_direct(resent, back, back_sems)

    def send_edges(back, beside, edge_sems):
        last, first = back.at[pl.ds(count - PARTS, PARTS)], back.at[pl.ds(0, PARTS)]
        return both_ways(last, first, beside, edge_sems, *bands)

    late_came()
    late = filtered(got_late)
    quarter = late.shape[0] // 4
    late_rows[...] = jnp.concatenate(
        [late[i * quarter : (i + 1) * quarter] for i in range(4)], axis=1
    )
    halo_came = both_ways(late_rows, late_rows, late_beside, sems[4], *rows)
    early_came()
    early_back = send_back(filtered(got_early), resent_early, back_early, sems[2])

    def unpacked(value):
        return jnp.concatenate([value[:, i * SHARE : (i + 1) * SHARE] for i in range(4)], axis=0)

    parts = blocks(late)
    west = jnp.concatenate([shifted(parts[-1], True)] + parts[:-1], axis=0)
    east = jnp.concatenate(parts[1:] + [shifted(parts[0], False)], axis=0)
    moved = coefs[:, 0:1] * late + coefs[:, 1:2] * west + coefs[:, 2:3] * east
    halo_came()
    moved = moved + coefs[:, 3:4] * unpacked(late_beside[0])
    moved = moved + coefs[:, 4:5] * unpacked(late_beside[1])
    late_back = send_back(product(matrix[...], moved), resent_late, back_late, sems[3])
    early_back()
    early_edges = send_edges(back_early, beside_early, sems[5])
    late_back()
    late_edges = send_edges(back_late, beside_late, sems[6])
    early_edges()
    late_edges()


GROUPS = 4


def call(kernel, number, outs, scratch, sems, *args):
    in_vmem = pl.BlockSpec(memory_space=pltpu.VMEM)
    return pl.pallas_call(
        kernel,
        out_shape=tuple(jax.ShapeDtypeStruct(shape, jnp.float32) for shape in outs),
        in_specs=[in_vmem] * len(args),
        out_specs=(in_vmem,) * len(outs),
        scratch_shapes=[pltpu.VMEM(shape, jnp.float32) for shape in scratch]
        + [pltpu.SemaphoreType.DMA((n,)) for n in sems],
        compiler_params=pltpu.CompilerParams(
            collective_id=number, has_side_effects=True, vmem_limit_bytes=48 * 1024 * 1024
        ),
    )(*args)


def by_groups(value):
    count, width = value.shape
    return value.reshape(GROUPS, count // GROUPS, 1, width)


def filter_factors(row, circle, lat_rows):
    half = circle // 2
    waves = np.concatenate([np.arange(half + 1), np.arange(1, half)])
    cells = np.arange(circle).reshape(-1, LON_DEV).T.reshape(1, circle)
    phase = waves[:, None] * cells % circle * (2.0 * math.pi / circle)
    basis = np.where(np.arange(circle)[:, None] <= half, np.cos(phase), np.sin(phase))
    basis = basis.astype(np.float32)
    coslat = jnp.cos((row.astype(jnp.float32) + 0.5) * (math.pi / lat_rows) - 0.5 * math.pi)
    sines = np.sin(waves * (math.pi / circle)).astype(np.float32)
    response = coslat / jnp.maximum(HALF_ROOT * sines, coslat)
    inverse = np.where((waves == 0) | (waves == half), 1.0, 2.0).astype(np.float32) / circle
    return jnp.asarray(basis.T), jnp.asarray(basis), (response * inverse)[None, :]


def filter_matrix(left_ref, right_ref, weight_ref, matrix_ref):
    block = matrix_ref.shape[0] // 4

    @pl.loop(0, 4)
    def _(i):
        rows = pl.ds(pl.multiple_of(i * block, block), block)
        matrix_ref[rows, :] = jnp.dot(
            left_ref[rows, :] * weight_ref[...],
            right_ref[...],
            precision=HIGHEST,
            preferred_element_type=jnp.float32,
        )


def channel_columns(table_ref, coupling_ref, once_ref, twice_ref):
    def couple(value):
        return value + jnp.dot(
            value,
            coupling_ref[...],
            precision=HIGHEST,
            preferred_element_type=jnp.float32,
        )

    once = couple(table_ref[...])
    once_ref[...] = once
    twice_ref[...] = couple(once)


def per_device(
    zonal, merid, diffuse, coupling, table, obs_dep, obs_frac, obs_owner, obs_lon, obs_lat, obs_chan
):
    lon_groups = lax.axis_size("lon")
    lat_groups = lax.axis_size("lat")
    columns = FIELDS * LEV
    circle = LON_DEV * lon_groups
    lat_rows = LAT_DEV * lat_groups
    lat_index = lax.axis_index("lat")
    own_row = lat_index * LAT_DEV + lax.axis_index("lon") // PARTS
    factors = filter_factors(own_row, circle, lat_rows)

    steps, rows = obs_dep.shape
    dest_ids = jnp.arange(lon_groups, dtype=jnp.int32)
    chosen = (obs_owner == dest_ids).astype(jnp.float32)
    earlier = jnp.arange(rows)[:, None] > jnp.arange(rows)[None, :]
    before = lax.dot_general(
        jnp.broadcast_to(earlier.astype(jnp.float32), (steps, rows, rows)),
        chosen,
        (((2,), (1,)), ((0,), (0,))),
    )
    rank = jnp.sum(before * chosen, axis=2)[:, :, None]
    in_slot = rank == jnp.arange(CAP, dtype=jnp.float32)
    details = [
        obs_dep,
        obs_frac[:, :, 0],
        obs_frac[:, :, 1],
        obs_lon.astype(jnp.float32),
        obs_lat.astype(jnp.float32),
        obs_chan.astype(jnp.float32),
    ]
    slotted = jnp.concatenate([jnp.where(in_slot, d[:, :, None], 0.0) for d in details], axis=2)
    sent = lax.dot_general(chosen, slotted, (((1,), (1,)), ((0,), (0,))), precision=HIGHEST)
    by_row = [jnp.repeat(c.T, PARTS, axis=0) for c in (zonal, merid, diffuse)]
    spare = jnp.zeros((lon_groups, 8), jnp.float32)
    sent = by_groups(jnp.concatenate([sent[0], sent[1]] + by_row + [spare], axis=1))
    turned = (sent.shape[1], sent.shape[0]) + sent.shape[2:]
    got, matrix = call(
        details_kernel, 0, (sent.shape, (circle, circle)), (turned,), (5,), sent, *factors
    )
    got = got.reshape(lon_groups, -1)

    cells = jnp.arange(LAT_DEV * (LON_DEV + 1), dtype=jnp.int32)
    cell_lat = (cells // (LON_DEV + 1)).astype(jnp.float32)
    cell_lon = (cells % (LON_DEV + 1)).astype(jnp.float32)
    items = jnp.arange(PARTS * ITEMS, dtype=jnp.int32)
    item_step = items // NCHAN
    item_chan = (items % NCHAN).astype(jnp.float32)
    weights, picks = [], []
    for step_id in range(steps):
        start = step_id * 6 * CAP
        dep, along, across, lon, lat, chan = (
            got[:, start + f * CAP : start + (f + 1) * CAP][:, :, None] for f in range(6)
        )
        lon_part = jnp.where(cell_lon == lon, 1.0 - along, 0.0)
        lon_part = lon_part + jnp.where(cell_lon == lon + 1.0, along, 0.0)
        lat_part = jnp.where(cell_lat == lat, 1.0 - across, 0.0)
        lat_part = lat_part + jnp.where(cell_lat == lat + 1.0, across, 0.0)
        weights.append((lon_part * lat_part).reshape(lon_groups * CAP, -1))
        hit = (item_chan == chan) & (item_step == step_id)
        picks.append(jnp.where(hit, dep, 0.0).reshape(lon_groups * CAP, -1))
    forcing = contract_first(jnp.concatenate(weights), jnp.concatenate(picks), HIGHEST)

    pieces = forcing.reshape(LAT_DEV, LON_DEV + 1, 2, PARTS, SHARE).transpose(2, 0, 3, 1, 4)
    pieces = pieces.reshape(2, lon_groups, 1, -1)
    pieces = jnp.pad(pieces, ((0, 0), (0, 0), (0, 0), (0, 3 * SHARE)))
    first_coef = 12 * CAP
    own_zonal, own_merid, own_diffuse = (
        got[:, first_coef + n * LON_DEV : first_coef + (n + 1) * LON_DEV].T.reshape(circle)
        for n in range(3)
    )
    own_row = jnp.full((circle,), own_row)
    coefs = [
        1.0 - 4.0 * own_diffuse,
        own_diffuse - 0.5 * own_zonal,
        own_diffuse + 0.5 * own_zonal,
        jnp.where(own_row > 0, own_diffuse - 0.5 * own_merid, 0.0),
        jnp.where(own_row < lat_rows - 1, own_diffuse + 0.5 * own_merid, 0.0),
    ]

    packed = (circle // 4, 4 * SHARE)
    piece = pieces.shape[1:]
    edge = (2, PARTS) + piece[1:]
    *blocks, once, twice = call(
        steps_kernel,
        1,
        (piece, piece, edge, edge, table.shape, table.shape),
        (piece, piece, packed, (2,) + packed, piece, piece),
        (3, 3, 3, 3, 4, 4, 4),
        pieces[0],
        pieces[1],
        matrix,
        jnp.stack(coefs, axis=1),
        table,
        coupling.T,
    )
    inside = jnp.array([lat_index > 0, lat_index < lat_groups - 1])[:, None, None]
    extended = []
    for back, beside in zip(blocks[:2], blocks[2:]):
        beside = jnp.where(inside, beside.reshape(2, PARTS, -1), 0.0)
        back = jnp.concatenate([beside[0], back.reshape(lon_groups, -1), beside[1]], axis=0)
        back = back[:, : (LON_DEV + 2) * SHARE]
        back = back.reshape(LAT_DEV + 2, PARTS, LON_DEV + 2, SHARE).transpose(2, 0, 1, 3)
        extended.append(back.reshape((LON_DEV + 2) * (LAT_DEV + 2), NCHAN))
    cube = jnp.dot(
        jnp.concatenate(extended, axis=1),
        jnp.concatenate([once, twice], axis=0),
        precision=HIGHEST,
    ).reshape(LON_DEV + 2, LAT_DEV + 2, columns)
    diffusion = diffuse[:, :, None]
    eastward = 0.5 * zonal[:, :, None]
    northward = 0.5 * merid[:, :, None]
    result = (1.0 - 4.0 * diffusion) * cube[1:-1, 1:-1]
    result = result + (diffusion - eastward) * cube[:-2, 1:-1]
    result = result + (diffusion + eastward) * cube[2:, 1:-1]
    result = result + (diffusion - northward) * cube[1:-1, :-2]
    result = result + (diffusion + northward) * cube[1:-1, 2:]
    return result.reshape(LON_DEV, LAT_DEV * columns)


def solution(mesh):
    return jax.shard_map(
        per_device,
        mesh=mesh,
        in_specs=(
            P("lon", "lat"),
            P("lon", "lat"),
            P("lon", "lat"),
            P(),
            P(),
            P(None, ("lon", "lat")),
            P(None, ("lon", "lat"), None),
            P(None, ("lon", "lat"), None),
            P(None, ("lon", "lat")),
            P(None, ("lon", "lat")),
            P(None, ("lon", "lat")),
        ),
        out_specs=P("lon", "lat"),
        check_vma=False,
    )
```

```python
import functools
import math

import jax
import jax.numpy as jnp
import numpy as np
from jax import lax
from jax.experimental import pallas as pl
from jax.experimental.pallas import tpu as pltpu
from jax.sharding import PartitionSpec as P

FIELDS = 5
LEV = 72
NCHAN = 128
LON_DEV = 8
LAT_DEV = 16
CAP = 8
PARTS = 4
SHARE = NCHAN // PARTS
ITEMS = 2 * SHARE


HALF_ROOT = 0.7071067811865476
HIGHEST = lax.Precision.HIGHEST


def contract_first(left, right, precision):
    return lax.dot_general(left, right, (((0,), (0,)), ((), ())), precision=precision)


def remote(source, target, send_sem, recv_sem, device):
    return pltpu.make_async_remote_copy(
        src_ref=source,
        dst_ref=target,
        send_sem=send_sem,
        recv_sem=recv_sem,
        device_id=device,
        device_id_type=pl.DeviceIdType.MESH,
    )


def greet(device):
    pl.semaphore_signal(
        pltpu.get_barrier_semaphore(),
        inc=1,
        device_id=device,
        device_id_type=pl.DeviceIdType.MESH,
    )


def in_group(shift, members):
    me = lax.axis_index("lon")
    place = lax.rem(lax.rem(me, members) + shift, members)
    return place, {"lon": me // members * members + place}


def across(shift, groups, members):
    me = lax.axis_index("lon")
    place = lax.rem(me // members + shift, groups)
    return place, {"lon": place * members + lax.rem(me, members)}


def greet_all(groups, members, more=()):
    @pl.loop(1, members)
    def _(shift):
        greet(in_group(shift, members)[1])

    @pl.loop(1, groups)
    def _(shift):
        greet(across(shift, groups, members)[1])

    for device in more:
        greet(device)
    pl.semaphore_wait(pltpu.get_barrier_semaphore(), members + groups - 2 + len(more))


def two_phases(sent, mid, got, sems, compute=None):
    near_send, near_recv, far_send, far_recv, own_sem = (sems.at[i] for i in range(5))
    groups, members = sent.shape[:2]
    me = lax.axis_index("lon")
    group, member = me // members, lax.rem(me, members)
    own = pltpu.make_async_copy(sent.at[:, member], mid.at[member], own_sem)
    own.start()

    @pl.loop(1, members)
    def _(shift):
        place, device = in_group(shift, members)
        remote(sent.at[:, place], mid.at[member], near_send, near_recv, device).start()

    if compute is not None:
        compute()
    own.wait()
    rest = mid.at[pl.ds(0, members - 1)]
    remote(rest, rest, near_send, near_recv, in_group(1, members)[1]).wait()

    own = pltpu.make_async_copy(mid.at[:, group], got.at[group], own_sem)
    own.start()

    @pl.loop(1, groups)
    def _(shift):
        place, device = across(shift, groups, members)
        remote(mid.at[:, place], got.at[group], far_send, far_recv, device).start()

    own.wait()
    rest = got.at[pl.ds(0, groups - 1)]
    remote(rest, rest, far_send, far_recv, across(1, groups, members)[1]).wait()


def peer(shift):
    count = lax.axis_size("lon")
    return lax.rem(lax.axis_index("lon") + shift, count)


def start_direct(sent, got, sems):
    me, count = lax.axis_index("lon"), lax.axis_size("lon")
    own = pltpu.make_async_copy(sent.at[me], got.at[me], sems.at[2])
    own.start()

    @pl.loop(1, count)
    def _(shift):
        place = peer(shift)
        remote(sent.at[place], got.at[me], sems.at[0], sems.at[1], {"lon": place}).start()

    def finish():
        own.wait()
        rest = got.at[pl.ds(0, count - 1)]
        remote(rest, rest, sems.at[0], sems.at[1], {"lon": peer(1)}).wait()

    return finish


def both_ways(up, down, landed, sems, above, below):
    first = remote(up, landed.at[0], sems.at[0], sems.at[1], above)
    second = remote(down, landed.at[1], sems.at[2], sems.at[3], below)
    first.start()
    second.start()

    def finish():
        first.wait()
        second.wait()

    return finish


def product(left, right):
    return jnp.dot(left, right, precision=HIGHEST, preferred_element_type=jnp.float32)


def details_kernel(sent, left, right, weight, got, matrix, mid, sems):
    greet_all(*sent.shape[:2])
    two_phases(sent, mid, got, sems, lambda: filter_matrix(left, right, weight, matrix))


def steps_kernel(
    sent_early,
    sent_late,
    matrix,
    coefs,
    table,
    coupling,
    back_early,
    back_late,
    beside_early,
    beside_late,
    once,
    twice,
    got_early,
    got_late,
    late_rows,
    late_beside,
    resent_early,
    resent_late,
    *sems,
):
    count = sent_early.shape[0]
    me, lat = lax.axis_index("lon"), lax.axis_index("lat")
    lat_groups = lax.axis_size("lat")
    bands = [{"lat": lax.rem(lat + shift, lat_groups)} for shift in (1, lat_groups - 1)]
    own_row = lat * LAT_DEV + me // PARTS
    lat_rows = lat_groups * LAT_DEV
    rows = [lax.rem(own_row + shift, lat_rows) for shift in (1, lat_rows - 1)]
    rows = [
        {"lon": lax.rem(row, LAT_DEV) * PARTS + lax.rem(me, PARTS), "lat": row // LAT_DEV}
        for row in rows
    ]

    @pl.loop(1, count)
    def _(shift):
        greet({"lon": peer(shift)})

    for device in bands + rows:
        greet(device)
    channel_columns(table, coupling, once, twice)
    pl.semaphore_wait(pltpu.get_barrier_semaphore(), count + 3)
    late_came = start_direct(sent_late, got_late, sems[0])
    early_came = start_direct(sent_early, got_early, sems[1])

    def blocks(value):
        return [value[i * count : (i + 1) * count] for i in range(LON_DEV)]

    def shifted(value, forward):
        if forward:
            return jnp.concatenate([value[-1:], value[:-1]], axis=0)
        return jnp.concatenate([value[1:], value[:1]], axis=0)

    def filtered(got):
        pieces = got[...].reshape(count, got.shape[2])
        circles = [pieces[:, i * SHARE : (i + 1) * SHARE] for i in range(LON_DEV + 1)]
        circles[0] = circles[0] + shifted(circles.pop(), True)
        return product(matrix[...], jnp.concatenate(circles, axis=0))

    def send_back(value, resent, back, back_sems):
        parts = blocks(value)
        wide = [shifted(parts[-1], True)] + parts + [shifted(parts[0], False)]
        wide = wide + [jnp.zeros_like(parts[0])] * (resent.shape[2] // SHARE - len(wide))
        resent[...] = jnp.concatenate(wide, axis=1).reshape(resent.shape)
        return start_direct(resent, back, back_sems)

    def send_edges(back, beside, edge_sems):
        last, first = back.at[pl.ds(count - PARTS, PARTS)], back.at[pl.ds(0, PARTS)]
        return both_ways(last, first, beside, edge_sems, *bands)

    late_came()
    late = filtered(got_late)
    quarter = late.shape[0] // 4
    late_rows[...] = jnp.concatenate(
        [late[i * quarter : (i + 1) * quarter] for i in range(4)], axis=1
    )
    halo_came = both_ways(late_rows, late_rows, late_beside, sems[4], *rows)
    early_came()
    early_back = send_back(filtered(got_early), resent_early, back_early, sems[2])

    def unpacked(value):
        return jnp.concatenate([value[:, i * SHARE : (i + 1) * SHARE] for i in range(4)], axis=0)

    parts = blocks(late)
    west = jnp.concatenate([shifted(parts[-1], True)] + parts[:-1], axis=0)
    east = jnp.concatenate(parts[1:] + [shifted(parts[0], False)], axis=0)
    moved = coefs[:, 0:1] * late + coefs[:, 1:2] * west + coefs[:, 2:3] * east
    halo_came()
    moved = moved + coefs[:, 3:4] * unpacked(late_beside[0])
    moved = moved + coefs[:, 4:5] * unpacked(late_beside[1])
    late_back = send_back(product(matrix[...], moved), resent_late, back_late, sems[3])
    early_back()
    early_edges = send_edges(back_early, beside_early, sems[5])
    late_back()
    late_edges = send_edges(back_late, beside_late, sems[6])
    early_edges()
    late_edges()


GROUPS = 4


def call(kernel, number, outs, scratch, sems, *args):
    in_vmem = pl.BlockSpec(memory_space=pltpu.VMEM)
    return pl.pallas_call(
        kernel,
        out_shape=tuple(jax.ShapeDtypeStruct(shape, jnp.float32) for shape in outs),
        in_specs=[in_vmem] * len(args),
        out_specs=(in_vmem,) * len(outs),
        scratch_shapes=[pltpu.VMEM(shape, jnp.float32) for shape in scratch]
        + [pltpu.SemaphoreType.DMA((n,)) for n in sems],
        compiler_params=pltpu.CompilerParams(
            collective_id=number, has_side_effects=True, vmem_limit_bytes=48 * 1024 * 1024
        ),
    )(*args)


def by_groups(value):
    count, width = value.shape
    return value.reshape(GROUPS, count // GROUPS, 1, width)


def filter_factors(row, circle, lat_rows):
    half = circle // 2
    waves = np.concatenate([np.arange(half + 1), np.arange(1, half)])
    cells = np.arange(circle).reshape(-1, LON_DEV).T.reshape(1, circle)
    phase = waves[:, None] * cells % circle * (2.0 * math.pi / circle)
    basis = np.where(np.arange(circle)[:, None] <= half, np.cos(phase), np.sin(phase))
    basis = basis.astype(np.float32)
    coslat = jnp.cos((row.astype(jnp.float32) + 0.5) * (math.pi / lat_rows) - 0.5 * math.pi)
    sines = np.sin(waves * (math.pi / circle)).astype(np.float32)
    response = coslat / jnp.maximum(HALF_ROOT * sines, coslat)
    inverse = np.where((waves == 0) | (waves == half), 1.0, 2.0).astype(np.float32) / circle
    return jnp.asarray(basis.T), jnp.asarray(basis), (response * inverse)[None, :]


def filter_matrix(left_ref, right_ref, weight_ref, matrix_ref):
    block = matrix_ref.shape[0] // 4

    @pl.loop(0, 4)
    def _(i):
        rows = pl.ds(pl.multiple_of(i * block, block), block)
        matrix_ref[rows, :] = jnp.dot(
            left_ref[rows, :] * weight_ref[...],
            right_ref[...],
            precision=HIGHEST,
            preferred_element_type=jnp.float32,
        )


def channel_columns(table_ref, coupling_ref, once_ref, twice_ref):
    def couple(value):
        return value + jnp.dot(
            value,
            coupling_ref[...],
            precision=HIGHEST,
            preferred_element_type=jnp.float32,
        )

    once = couple(table_ref[...])
    once_ref[...] = once
    twice_ref[...] = couple(once)


def per_device(
    zonal, merid, diffuse, coupling, table, obs_dep, obs_frac, obs_owner, obs_lon, obs_lat, obs_chan
):
    lon_groups = lax.axis_size("lon")
    lat_groups = lax.axis_size("lat")
    columns = FIELDS * LEV
    circle = LON_DEV * lon_groups
    lat_rows = LAT_DEV * lat_groups
    lat_index = lax.axis_index("lat")
    own_row = lat_index * LAT_DEV + lax.axis_index("lon") // PARTS
    factors = filter_factors(own_row, circle, lat_rows)

    steps, rows = obs_dep.shape
    dest_ids = jnp.arange(lon_groups, dtype=jnp.int32)
    chosen = (obs_owner == dest_ids).astype(jnp.float32)
    earlier = jnp.arange(rows)[:, None] > jnp.arange(rows)[None, :]
    before = lax.dot_general(
        jnp.broadcast_to(earlier.astype(jnp.float32), (steps, rows, rows)),
        chosen,
        (((2,), (1,)), ((0,), (0,))),
    )
    rank = jnp.sum(before * chosen, axis=2)[:, :, None]
    in_slot = rank == jnp.arange(CAP, dtype=jnp.float32)
    details = [
        obs_dep,
        obs_frac[:, :, 0],
        obs_frac[:, :, 1],
        *jnp.stack([obs_lon, obs_lat, obs_chan]).astype(jnp.float32),
    ]
    slotted = jnp.concatenate([jnp.where(in_slot, d[:, :, None], 0.0) for d in details], axis=2)
    sent = lax.dot_general(chosen, slotted, (((1,), (1,)), ((0,), (0,))), precision=HIGHEST)
    by_row = jnp.stack([zonal, merid, diffuse]).transpose(2, 0, 1).reshape(LAT_DEV, 3 * LON_DEV)
    by_row = jnp.repeat(by_row, PARTS, axis=0)
    spare = jnp.zeros((lon_groups, 8), jnp.float32)
    sent = by_groups(jnp.concatenate([sent[0], sent[1], by_row, spare], axis=1))
    turned = (sent.shape[1], sent.shape[0]) + sent.shape[2:]
    got, matrix = call(
        details_kernel, 0, (sent.shape, (circle, circle)), (turned,), (5,), sent, *factors
    )
    got = got.reshape(lon_groups, -1)

    cells = jnp.arange(LAT_DEV * (LON_DEV + 1), dtype=jnp.int32)
    cell_lat = (cells // (LON_DEV + 1)).astype(jnp.float32)
    cell_lon = (cells % (LON_DEV + 1)).astype(jnp.float32)
    items = jnp.arange(PARTS * ITEMS, dtype=jnp.int32)
    item_step = items // NCHAN
    item_chan = (items % NCHAN).astype(jnp.float32)
    weights, picks = [], []
    for step_id in range(steps):
        start = step_id * 6 * CAP
        dep, along, across, lon, lat, chan = (
            got[:, start + f * CAP : start + (f + 1) * CAP][:, :, None] for f in range(6)
        )
        lon_part = jnp.where(cell_lon == lon, 1.0 - along, 0.0)
        lon_part = lon_part + jnp.where(cell_lon == lon + 1.0, along, 0.0)
        lat_part = jnp.where(cell_lat == lat, 1.0 - across, 0.0)
        lat_part = lat_part + jnp.where(cell_lat == lat + 1.0, across, 0.0)
        weights.append((lon_part * lat_part).reshape(lon_groups * CAP, -1))
        hit = (item_chan == chan) & (item_step == step_id)
        picks.append(jnp.where(hit, dep, 0.0).reshape(lon_groups * CAP, -1))
    forcing = contract_first(jnp.concatenate(weights), jnp.concatenate(picks), HIGHEST)

    pieces = forcing.reshape(LAT_DEV, LON_DEV + 1, 2, PARTS, SHARE).transpose(2, 0, 3, 1, 4)
    pieces = pieces.reshape(2, lon_groups, 1, -1)
    pieces = jnp.pad(pieces, ((0, 0), (0, 0), (0, 0), (0, 3 * SHARE)))
    first_coef = 12 * CAP
    own = got[:, first_coef : first_coef + 3 * LON_DEV].reshape(lon_groups, 3, LON_DEV)
    own_zonal, own_merid, own_diffuse = own.transpose(1, 2, 0).reshape(3, circle)
    own_row = jnp.full((circle,), own_row)
    coefs = [
        1.0 - 4.0 * own_diffuse,
        own_diffuse - 0.5 * own_zonal,
        own_diffuse + 0.5 * own_zonal,
        jnp.where(own_row > 0, own_diffuse - 0.5 * own_merid, 0.0),
        jnp.where(own_row < lat_rows - 1, own_diffuse + 0.5 * own_merid, 0.0),
    ]

    packed = (circle // 4, 4 * SHARE)
    piece = pieces.shape[1:]
    edge = (2, PARTS) + piece[1:]
    *blocks, once, twice = call(
        steps_kernel,
        1,
        (piece, piece, edge, edge, table.shape, table.shape),
        (piece, piece, packed, (2,) + packed, piece, piece),
        (3, 3, 3, 3, 4, 4, 4),
        pieces[0],
        pieces[1],
        matrix,
        jnp.stack(coefs, axis=1),
        table,
        coupling.T,
    )
    inside = jnp.array([lat_index > 0, lat_index < lat_groups - 1])[:, None, None]
    extended = []
    for back, beside in zip(blocks[:2], blocks[2:]):
        beside = jnp.where(inside, beside.reshape(2, PARTS, -1), 0.0)
        back = jnp.concatenate([beside[0], back.reshape(lon_groups, -1), beside[1]], axis=0)
        back = back[:, : (LON_DEV + 2) * SHARE]
        back = back.reshape(LAT_DEV + 2, PARTS, LON_DEV + 2, SHARE).transpose(2, 0, 1, 3)
        extended.append(back.reshape((LON_DEV + 2) * (LAT_DEV + 2), NCHAN))
    cube = jnp.dot(
        jnp.concatenate(extended, axis=1),
        jnp.concatenate([once, twice], axis=0),
        precision=HIGHEST,
    ).reshape(LON_DEV + 2, LAT_DEV + 2, columns)
    diffusion = diffuse[:, :, None]
    eastward = 0.5 * zonal[:, :, None]
    northward = 0.5 * merid[:, :, None]
    result = (1.0 - 4.0 * diffusion) * cube[1:-1, 1:-1]
    result = result + (diffusion - eastward) * cube[:-2, 1:-1]
    result = result + (diffusion + eastward) * cube[2:, 1:-1]
    result = result + (diffusion - northward) * cube[1:-1, :-2]
    result = result + (diffusion + northward) * cube[1:-1, 2:]
    return result.reshape(LON_DEV, LAT_DEV * columns)


def solution(mesh):
    return jax.shard_map(
        per_device,
        mesh=mesh,
        in_specs=(
            P("lon", "lat"),
            P("lon", "lat"),
            P("lon", "lat"),
            P(),
            P(),
            P(None, ("lon", "lat")),
            P(None, ("lon", "lat"), None),
            P(None, ("lon", "lat"), None),
            P(None, ("lon", "lat")),
            P(None, ("lon", "lat")),
            P(None, ("lon", "lat")),
        ),
        out_specs=P("lon", "lat"),
        check_vma=False,
    )
```
